128 devices in a mesh: cand: 4 (over x_lo, core), seq: 32 (over x_hi, y, z).
Axes of the slice: x: 4 (x_hi: 2, x_lo: 2; x = x_hi * 2 + x_lo), y: 4, z: 4, core: 2. Of those that a mesh axis runs over, the one named last changes fastest.
Arguments:
- hyena_query: bfloat16 [4, 4096, 4096], P('cand', 'seq'), may hold values from -6 to 6
- hyena_key: bfloat16 [4, 4096, 4096], P('cand', 'seq'), may hold values from -6 to 6
- hyena_value: bfloat16 [4, 4096, 4096], P('cand', 'seq'), may hold values from -6 to 6
- hyena_filters: float32 [128, 256], replicated, may hold values from -0.5 to 0.5
- context_tail: bfloat16 [127, 4096], replicated, may hold values from -6 to 6
- cont_queries: bfloat16 [4, 4096, 32, 128], P('cand', 'seq'), may hold values from -100 to 100
- cont_keys: bfloat16 [4, 4096, 32, 128], P('cand', 'seq'), may hold values from -5 to 5
- cont_values: bfloat16 [4, 4096, 32, 128], P('cand', 'seq'), may hold values from -6 to 6
- context_keys: bfloat16 [3072, 32, 128], P('seq'), may hold values from -6 to 6
- context_values: bfloat16 [3072, 32, 128], P('seq'), may hold values from -6 to 6
- lengths: int32 [4], P('cand'), may hold values from 1024 to 4096, as said below
Outputs:
- hyena_out: bfloat16 [4, 4096, 4096], P('cand', 'seq')
- attention_out: bfloat16 [4, 4096, 32, 128], P('cand', 'seq')
The draws below stay inside these ranges and needn't reach their ends.
Inputs may be any that keep to these rules, and one draw needn't show every extreme that they name: `lengths`: positions of a candidate at or past its length are padding; some candidate has all 4096 positions valid.
All inputs are finite; a program needn't handle non-finite values.
Results may differ from the reference program's by a relative error of at most 0.0049.
Values may be sent and summed in bfloat16 or wider, within the bound.
A program may use at most 64 MiB of HBM per device.

```python
import math
import jax
import jax.numpy as jnp
from jax import lax

CH = 4096
CH_GROUP = 16
FILT = 128
HEADS = 32
HD = 128
CAND = 4
LEN = 4096
CTX = 3072
FGROUPS = 256


def paired_draws(key):
    base = jax.random.fold_in(key, 11)
    key_query, key_key = jax.random.split(base, 2)
    shape = (CAND, LEN, HEADS, HD)
    queries = jnp.clip(2.5 * jax.random.normal(key_query, shape, jnp.float32), -12.0, 12.0)
    key_rows = jnp.clip(jax.random.normal(key_key, shape, jnp.float32), -5.0, 5.0)
    return (queries, key_rows)


def draw_cont_queries(key, part):
    return paired_draws(key)[0].astype(jnp.bfloat16)


def draw_cont_keys(key, part):
    return paired_draws(key)[1].astype(jnp.bfloat16)


def draw_lengths(key, part):
    key_first, key_second = jax.random.split(jax.random.fold_in(key, 5))
    drawn = jax.random.randint(key_first, (CAND,), LEN // 4, LEN + 1)
    chosen = jax.random.randint(key_second, (), 0, CAND)
    return jnp.where(jnp.arange(CAND) == chosen, LEN, drawn).astype(jnp.int32)


def block_levels(own_key, extent, cuts, low, top_value):
    def one(dim, shards_of):
        steps = jax.random.uniform(jax.random.fold_in(jax.random.fold_in(own_key, 6), dim), (shards_of,), jnp.float32, low / len(cuts), top_value / len(cuts))
        return jnp.repeat(jnp.exp(steps), extent[dim] // shards_of).reshape((-1,) + (1,) * (len(extent) - dim - 1))

    gain = one(*cuts[0])
    for cut in cuts[1:]:
        gain = gain * one(*cut)
    return gain


def scatter_about(own_key, extent, scale, most, shards=(), held_as=jnp.bfloat16):
    values = jax.random.normal(own_key, extent, jnp.float32) * scale
    if len(shards) > 0:
        values = block_levels(own_key, extent, shards, -0.22, 0.18) * values
    return jnp.clip(values, min=-most, max=most).astype(held_as)


def setup_inputs(seed: int = 0) -> dict:
    key_of = jax.random.split(jax.random.key(seed), 12)
    return {
        "hyena_query": scatter_about(key_of[0], (CAND, LEN, CH), 1.0, 6.0, ((0, 4), (1, 32))),
        "hyena_key": scatter_about(key_of[1], (CAND, LEN, CH), 1.0, 6.0, ((0, 4), (1, 32))),
        "hyena_value": scatter_about(key_of[2], (CAND, LEN, CH), 1.0, 6.0, ((0, 4), (1, 32))),
        "hyena_filters": scatter_about(key_of[3], (FILT, FGROUPS), FILT ** -0.5, 0.5, (), jnp.float32),
        "context_tail": scatter_about(key_of[4], (FILT - 1, CH), 1.0, 6.0),
        "cont_queries": draw_cont_queries(jax.random.fold_in(key_of[11], 71), 0),
        "cont_keys": draw_cont_keys(jax.random.fold_in(key_of[11], 71), 0),
        "cont_values": scatter_about(key_of[7], (CAND, LEN, HEADS, HD), 1.0, 6.0, ((0, 4), (1, 32))),
        "context_keys": scatter_about(key_of[8], (CTX, HEADS, HD), 1.0, 6.0, ((0, 32),)),
        "context_values": scatter_about(key_of[9], (CTX, HEADS, HD), 1.0, 6.0, ((0, 32),)),
        "lengths": draw_lengths(jax.random.fold_in(key_of[11], 71), 0),
    }


masked_score = -1e+30

def reference(hyena_query, hyena_key, hyena_value, hyena_filters, context_tail, cont_queries, cont_keys, cont_values, context_keys, context_values, lengths):
    per_channel = jnp.repeat(hyena_filters, CH_GROUP, axis=1)
    places = jnp.arange(LEN)

    def hyena_one(operands):
        query_rows, key_rows, value_rows, length_one = operands
        product = (key_rows.astype(jnp.float32) * value_rows.astype(jnp.float32)).astype(jnp.bfloat16)
        extended = jnp.concatenate([context_tail, product], axis=0).astype(jnp.float32)

        def add_tap(offset, running):
            start = (FILT - 1 - offset).astype(jnp.int32)
            return running + per_channel[offset][None, :] * lax.dynamic_slice_in_dim(extended, start, LEN, 0)
        convolved = lax.fori_loop(0, FILT, add_tap, jnp.zeros((LEN, CH), jnp.float32))
        keep = places < length_one
        return jnp.where(keep[:, None], query_rows.astype(jnp.float32) * convolved, 0.0).astype(jnp.bfloat16)
    hyena_out = lax.map(hyena_one, (hyena_query, hyena_key, hyena_value, lengths))
    block_rows = min(512, LEN)
    count = LEN // block_rows
    scaling = 1.0 / math.sqrt(HD)

    def head_one(operands):
        query_rows, key_rows, value_rows, context_key_rows, context_value_rows = operands
        all_keys = jnp.concatenate([context_key_rows, key_rows], axis=0)
        all_values = jnp.concatenate([context_value_rows, value_rows], axis=0)

        def block_one(index):
            start = (index * block_rows).astype(jnp.int32)
            query_block = lax.dynamic_slice_in_dim(query_rows, start, block_rows, 0)
            scores = jnp.dot(query_block, all_keys.T, preferred_element_type=jnp.float32) * scaling
            query_places = index * block_rows + jnp.arange(block_rows)
            allowed = jnp.concatenate([jnp.ones((block_rows, CTX), jnp.bool_), places[None, :] <= query_places[:, None]], axis=1)
            scores = jnp.where(allowed, scores, masked_score)
            highest = lax.optimization_barrier(jnp.max(scores, axis=1, keepdims=True))
            weights = jnp.exp(scores - highest)
            totals = lax.optimization_barrier(jnp.sum(weights, axis=1))
            mixed = jnp.dot(weights.astype(jnp.bfloat16), all_values, preferred_element_type=jnp.float32)
            return mixed / totals[:, None]
        return lax.map(block_one, jnp.arange(count)).reshape(LEN, HD)

    def cand_one(operands):
        query_rows, key_rows, value_rows, length_one = operands
        result = lax.map(head_one, (query_rows.transpose(1, 0, 2), key_rows.transpose(1, 0, 2), value_rows.transpose(1, 0, 2), context_keys.transpose(1, 0, 2), context_values.transpose(1, 0, 2)))
        result = result.transpose(1, 0, 2)
        keep = places < length_one
        return jnp.where(keep[:, None, None], result, 0.0).astype(jnp.bfloat16)
    attention_out = lax.map(cand_one, (cont_queries, cont_keys, cont_values, lengths))
    return (hyena_out, attention_out)
```

```python
import functools
import math

import jax
import jax.numpy as jnp
from jax import lax
from jax.experimental import pallas as pl
from jax.experimental.pallas import tpu as pltpu
from jax.sharding import PartitionSpec as P

F32 = jnp.float32
BF16 = jnp.bfloat16
MESH = pl.DeviceIdType.MESH
NT = (((1,), (1,)), ((), ()))
NN = (((1,), (0,)), ((), ()))
TN = (((0,), (0,)), ((), ()))
LOW = -1e30


def dot(a, b, dims):
    return lax.dot_general(a, b, dims, preferred_element_type=F32)


def fused(
    n, groups_per_tile, scale,
    hq_hbm, hk_hbm, hv_hbm, filt_ref, tail_hbm, q_hbm, k_hbm, v_hbm, ck_hbm, cv_hbm, len_ref,
    hy_ref, att_ref,
    hq, hk, hv, tail, ext, ring,
    q_in, k_in, v_in, ck_in, cv_in, wide,
    q_out, k_out, v_out, ck_out, cv_out,
    q_all, k_all, v_all, ck_all, cv_all,
    m_s, l_s, acc_s, o_out, o_in,
    load_sem, send_sem, recv_sem,
):
    rows, heads, width = q_in.shape
    half_rows = ck_in.shape[0]
    length_all = n * rows
    me = lax.axis_index("seq")
    cand = lax.axis_index("cand")
    half = lax.rem(cand, 2)
    partner = cand + 1 - 2 * half

    barrier = pltpu.get_barrier_semaphore()

    def greet(i, _):
        pl.semaphore_signal(
            barrier, inc=1, device_id=(cand, lax.rem(me + i, n)), device_id_type=MESH
        )
        return 0

    lax.fori_loop(1, n, greet, 0)
    pl.semaphore_signal(barrier, inc=1, device_id=(partner, me), device_id_type=MESH)

    ctx_rows = pl.ds(half * half_rows, half_rows)
    loads = [
        pltpu.make_async_copy(ck_hbm.at[ctx_rows], ck_in, load_sem.at[0]),
        pltpu.make_async_copy(cv_hbm.at[ctx_rows], cv_in, load_sem.at[1]),
        pltpu.make_async_copy(q_hbm.at[0], q_in, load_sem.at[2]),
        pltpu.make_async_copy(k_hbm.at[0], k_in, load_sem.at[3]),
        pltpu.make_async_copy(v_hbm.at[0], v_in, load_sem.at[4]),
        pltpu.make_async_copy(hk_hbm.at[0], hk, load_sem.at[5]),
        pltpu.make_async_copy(hv_hbm.at[0], hv, load_sem.at[6]),
        pltpu.make_async_copy(hq_hbm.at[0], hq, load_sem.at[7]),
        pltpu.make_async_copy(tail_hbm, tail, load_sem.at[8]),
    ]
    for copy in loads:
        copy.start()

    def by_head(src, dst):
        count = src.shape[0]
        wide[: count * heads, :] = src[...].astype(F32).reshape(count * heads, width)
        for h in range(heads):
            dst[h] = wide[pl.ds(h, count, stride=heads), :].astype(BF16)

    def scatter(src, dst_at, index):
        own = pltpu.make_async_copy(src.at[me], dst_at(me), recv_sem.at[index])
        own.start()

        def send(i, _):
            p = lax.rem(me + i, n)
            pltpu.make_async_remote_copy(
                src_ref=src.at[p], dst_ref=dst_at(me), send_sem=send_sem.at[index],
                recv_sem=recv_sem.at[index], device_id=(cand, p), device_id_type=MESH,
            ).start()
            return 0

        lax.fori_loop(1, n, send, 0)

    def received(whole, index):
        pltpu.make_async_copy(whole, whole, recv_sem.at[index]).wait()

    def sent(part, index):
        pltpu.make_async_copy(part, part, send_sem.at[index]).wait()

    loads[0].wait()
    by_head(ck_in, ck_out)
    loads[1].wait()
    by_head(cv_in, cv_out)
    pl.semaphore_wait(barrier, n)
    scatter(ck_out, lambda s: ck_all.at[half, s], 0)
    scatter(cv_out, lambda s: cv_all.at[half, s], 1)
    loads[2].wait()
    by_head(q_in, q_out)
    scatter(q_out, lambda s: q_all.at[s], 2)
    loads[3].wait()
    by_head(k_in, k_out)
    scatter(k_out, lambda s: k_all.at[s], 3)
    loads[4].wait()
    by_head(v_in, v_out)
    scatter(v_out, lambda s: v_all.at[s], 4)

    loads[5].wait()
    loads[6].wait()
    ext[1] = (hk[...].astype(F32) * hv[...].astype(F32)).astype(BF16)

    def halo(to):
        return pltpu.make_async_remote_copy(
            src_ref=ext.at[1], dst_ref=ext.at[0], send_sem=send_sem.at[5],
            recv_sem=recv_sem.at[5], device_id=(cand, to), device_id_type=MESH,
        )

    @pl.when(me + 1 < n)
    def _():
        halo(me + 1).start()

    loads[8].wait()

    taps = filt_ref.shape[0]
    turn_s = lax.broadcasted_iota(jnp.int32, (taps, taps), 0)
    turn_w = lax.broadcasted_iota(jnp.int32, (taps, taps), 1)
    turned = jnp.where((turn_s + turn_w) % taps == 0, 1.0, 0.0).astype(BF16)
    ring[...] = dot(filt_ref[...].astype(BF16), turned, TN)

    received(ck_all.at[half], 0)
    received(cv_all.at[half], 1)
    swaps = []
    for index, ref in ((6, ck_all), (7, cv_all)):
        swap = pltpu.make_async_remote_copy(
            src_ref=ref.at[half], dst_ref=ref.at[half], send_sem=send_sem.at[index],
            recv_sem=recv_sem.at[index], device_id=(partner, me), device_id_type=MESH,
        )
        swap.start()
        swaps.append(swap)
    for swap in swaps:
        swap.wait_recv()
    received(q_all, 2)

    def fold(state, query_block, key_rows, value_rows, mask=None):
        m, l, acc = state
        s = dot(query_block, key_rows, NT)
        if mask is not None:
            s = jnp.where(mask, s, LOW)
        top = jnp.maximum(m, jnp.max(s, axis=1, keepdims=True))
        w = jnp.exp2((s - top) * scale)
        shrink = jnp.exp2((m - top) * scale)
        l = l * shrink + jnp.sum(w, axis=1, keepdims=True)
        acc = acc * shrink + dot(w.astype(BF16), value_rows, NN)
        return top, l, acc

    block = min(512, length_all)
    per_block = block // rows
    blocks = length_all // block
    ctx_total = 2 * n * half_rows
    ctx_step = 1024 if ctx_total % 1024 == 0 else ctx_total
    q_flat = q_all.reshape(length_all, width)
    k_flat = k_all.reshape(length_all, width)
    v_flat = v_all.reshape(length_all, width)
    ck_flat = ck_all.reshape(ctx_total, width)
    cv_flat = cv_all.reshape(ctx_total, width)

    def over_context(i, _):
        at = pl.ds(pl.multiple_of(i * block, block), block)
        query_block = q_flat[at, :]
        state = (
            jnp.full((block, 1), LOW, F32), jnp.zeros((block, 1), F32), jnp.zeros((block, width), F32)
        )
        for j in range(ctx_total // ctx_step):
            part = slice(j * ctx_step, (j + 1) * ctx_step)
            state = fold(state, query_block, ck_flat[part, :], cv_flat[part, :])
        m_s[at, :], l_s[at, :], acc_s[at, :] = state
        return 0

    lax.fori_loop(0, blocks, over_context, 0)

    received(k_all, 3)
    received(v_all, 4)

    o_flat = o_out.reshape(length_all, width)
    row_at = lax.broadcasted_iota(jnp.int32, (block, block), 0)
    col_at = lax.broadcasted_iota(jnp.int32, (block, block), 1)
    causal = col_at <= row_at

    def over_pair(step, _):
        low = lax.rem(step + me, blocks // 2)
        high = blocks - 1 - low

        def visit(q_index, k_index, mask=None):
            at = pl.ds(pl.multiple_of(q_index * block, block), block)
            ks = pl.ds(pl.multiple_of(k_index * block, block), block)
            state = (m_s[at, :], l_s[at, :], acc_s[at, :])
            m_s[at, :], l_s[at, :], acc_s[at, :] = fold(
                state, q_flat[at, :], k_flat[ks, :], v_flat[ks, :], mask
            )

        for t in range(blocks - 1):
            first = t < low
            visit(jnp.where(first, low, high), jnp.where(first, t, t - low))
        for index in (low, high):
            visit(index, index, causal)
            at = pl.ds(pl.multiple_of(index * block, block), block)
            o_flat[at, :] = (acc_s[at, :] / l_s[at, :]).astype(BF16)
            for r in range(per_block):
                p = index * per_block + r

                @pl.when(p != me)
                def _():
                    pltpu.make_async_remote_copy(
                        src_ref=o_out.at[p], dst_ref=o_in.at[me], send_sem=send_sem.at[8],
                        recv_sem=recv_sem.at[8], device_id=(cand, p), device_id_type=MESH,
                    ).start()
        return 0

    lax.fori_loop(0, blocks // 2, over_pair, 0)
    pltpu.make_async_copy(o_out.at[me], o_in.at[me], recv_sem.at[8]).start()

    @pl.when(me == 0)
    def _():
        def shift(j, _):
            cols = pl.ds(pl.multiple_of(j * 512, 512), 512)
            held = tail[:, cols].astype(F32)
            ext[0, :, cols] = jnp.concatenate([jnp.zeros((1, 512), F32), held], axis=0).astype(BF16)
            return 0

        lax.fori_loop(0, tail.shape[1] // 512, shift, 0)

    @pl.when(me > 0)
    def _():
        halo(me).wait_recv()

    loads[7].wait()
    valid = len_ref[0] - me * rows
    out_row = lax.broadcasted_iota(jnp.int32, (rows, 128), 0)
    out_col = lax.broadcasted_iota(jnp.int32, (rows, 128), 1)
    keep = out_row < valid
    before = out_col > out_row
    lane_group = out_col // (128 // groups_per_tile)

    def filtered(j, _):
        cols = pl.ds(pl.multiple_of(j * 128, 128), 128)
        eight = ring[pl.ds(pl.multiple_of(j * groups_per_tile, groups_per_tile), groups_per_tile), :]
        earlier = []
        current = []
        for g in range(groups_per_tile):
            spread = jnp.broadcast_to(eight[g : g + 1, :], (rows, 128))
            turns = pltpu.roll(spread, 0, 1, stride=1, stride_axis=0)
            earlier.append(jnp.where(before, turns, 0.0).astype(BF16))
            current.append(jnp.where(before, 0.0, turns).astype(BF16))
        mats = jnp.concatenate(
            [jnp.concatenate(earlier, axis=0), jnp.concatenate(current, axis=0)], axis=1
        )
        stream = jnp.concatenate([ext[0, :, cols], ext[1, :, cols]], axis=0)
        every = dot(mats, stream, NN)
        mixed = every[:rows]
        for g in range(1, groups_per_tile):
            mixed = jnp.where(lane_group == g, every[g * rows : (g + 1) * rows], mixed)
        gated = jnp.where(keep, hq[:, cols].astype(F32) * mixed, 0.0)
        hy_ref[0, :, cols] = gated.astype(BF16)
        return 0

    lax.fori_loop(0, ext.shape[2] // 128, filtered, 0)

    received(o_in, 8)
    for h in range(heads):
        wide[pl.ds(h, rows, stride=heads), :] = o_in[h].astype(F32)
    position = lax.broadcasted_iota(jnp.int32, (rows, heads, width), 0)
    att_ref[0] = jnp.where(
        position < valid, wide[...].reshape(rows, heads, width), 0.0
    ).astype(BF16)

    for index, ref in ((0, ck_out), (1, cv_out), (2, q_out), (3, k_out), (4, v_out), (8, o_out)):
        sent(ref.at[pl.ds(0, n - 1)], index)

    @pl.when(me + 1 < n)
    def _():
        halo(me + 1).wait_send()

    for swap in swaps:
        swap.wait_send()


def local(
    hyena_query, hyena_key, hyena_value, hyena_filters, context_tail,
    cont_queries, cont_keys, cont_values, context_keys, context_values, lengths,
):
    n = lax.axis_size("seq")
    _, rows, channels = hyena_key.shape
    heads, width = cont_queries.shape[2:]
    half_rows = context_keys.shape[0] // 2
    taps, groups = hyena_filters.shape
    groups_per_tile = 128 * groups // channels
    length_all = n * rows
    scale = math.log2(math.e) / math.sqrt(width)
    hbm = pl.BlockSpec(memory_space=pl.ANY)
    vmem = pl.BlockSpec(memory_space=pltpu.VMEM)
    block = pltpu.VMEM((rows, heads, width), BF16)
    per_head = pltpu.VMEM((n, rows, width), BF16)
    half_block = pltpu.VMEM((half_rows, heads, width), BF16)
    half_heads = pltpu.VMEM((n, half_rows, width), BF16)
    both_halves = pltpu.VMEM((2, n, half_rows, width), BF16)
    stream = pltpu.VMEM((rows, channels), BF16)
    return pl.pallas_call(
        functools.partial(fused, n, groups_per_tile, scale),
        out_shape=(
            jax.ShapeDtypeStruct(hyena_query.shape, BF16),
            jax.ShapeDtypeStruct(cont_queries.shape, BF16),
        ),
        in_specs=[hbm, hbm, hbm, vmem, hbm, hbm, hbm, hbm, hbm, hbm,
                  pl.BlockSpec(memory_space=pltpu.SMEM)],
        out_specs=(vmem, vmem),
        scratch_shapes=[
            stream, stream, stream,
            pltpu.VMEM(context_tail.shape, BF16),
            pltpu.VMEM((2, rows, channels), BF16),
            pltpu.VMEM((groups, taps), F32),
            block, block, block, half_block, half_block,
            pltpu.VMEM((rows * heads, width), F32),
            per_head, per_head, per_head, half_heads, half_heads,
            per_head, per_head, per_head, both_halves, both_halves,
            pltpu.VMEM((length_all, 1), F32), pltpu.VMEM((length_all, 1), F32),
            pltpu.VMEM((length_all, width), F32),
            per_head, per_head,
            pltpu.SemaphoreType.DMA((9,)), pltpu.SemaphoreType.DMA((9,)), pltpu.SemaphoreType.DMA((9,)),
        ],
        compiler_params=pltpu.CompilerParams(
            collective_id=0, has_side_effects=True, vmem_limit_bytes=63 * 2**20
        ),
        name="fused",
    )(
        hyena_query, hyena_key, hyena_value, hyena_filters, context_tail,
        cont_queries, cont_keys, cont_values, context_keys, context_values, lengths,
    )


def solution(mesh):
    placed = (
        P("cand", "seq", None), P("cand", "seq", None), P("cand", "seq", None), P(), P(),
        P("cand", "seq", None, None), P("cand", "seq", None, None), P("cand", "seq", None, None),
        P("seq", None, None), P("seq", None, None), P("cand"),
    )
    return jax.shard_map(
        local, mesh=mesh, in_specs=placed,
        out_specs=(P("cand", "seq", None), P("cand", "seq", None, None)), check_vma=False,
    )
```

```python
import functools
import math

import jax
import jax.numpy as jnp
from jax import lax
from jax.experimental import pallas as pl
from jax.experimental.pallas import tpu as pltpu
from jax.sharding import PartitionSpec as P

F32 = jnp.float32
BF16 = jnp.bfloat16
MESH = pl.DeviceIdType.MESH
NT = (((1,), (1,)), ((), ()))
NN = (((1,), (0,)), ((), ()))
TN = (((0,), (0,)), ((), ()))
LOW = -1e30


def dot(a, b, dims):
    return lax.dot_general(a, b, dims, preferred_element_type=F32)


def fused(
    n, groups_per_tile, scale,
    hq_hbm, hk_hbm, hv_hbm, filt_ref, tail_hbm, q_hbm, k_hbm, v_hbm, ck_hbm, cv_hbm, len_ref,
    hy_ref, att_ref,
    hq, hk, hv, tail, ext, ring,
    q_in, k_in, v_in, ck_in, cv_in,
    q_out, k_out, v_out, ck_out, cv_out,
    q_all, k_all, v_all, ck_all, cv_all,
    m_s, l_s, acc_s, o_out, o_in,
    load_sem, send_sem, recv_sem,
):
    rows, heads, width = q_in.shape
    half_rows = ck_in.shape[0]
    length_all = n * rows
    me = lax.axis_index("seq")
    cand = lax.axis_index("cand")
    half = lax.rem(cand, 2)
    partner = cand + 1 - 2 * half

    barrier = pltpu.get_barrier_semaphore()

    def greet(i, _):
        pl.semaphore_signal(
            barrier, inc=1, device_id=(cand, lax.rem(me + i, n)), device_id_type=MESH
        )
        return 0

    lax.fori_loop(1, n, greet, 0)
    pl.semaphore_signal(barrier, inc=1, device_id=(partner, me), device_id_type=MESH)

    ctx_rows = pl.ds(half * half_rows, half_rows)
    loads = [
        pltpu.make_async_copy(ck_hbm.at[ctx_rows], ck_in, load_sem.at[0]),
        pltpu.make_async_copy(cv_hbm.at[ctx_rows], cv_in, load_sem.at[1]),
        pltpu.make_async_copy(q_hbm.at[0], q_in, load_sem.at[2]),
        pltpu.make_async_copy(k_hbm.at[0], k_in, load_sem.at[3]),
        pltpu.make_async_copy(v_hbm.at[0], v_in, load_sem.at[4]),
        pltpu.make_async_copy(hk_hbm.at[0], hk, load_sem.at[5]),
        pltpu.make_async_copy(hv_hbm.at[0], hv, load_sem.at[6]),
        pltpu.make_async_copy(hq_hbm.at[0], hq, load_sem.at[7]),
        pltpu.make_async_copy(tail_hbm, tail, load_sem.at[8]),
    ]
    for copy in loads:
        copy.start()

    perm_to = lax.broadcasted_iota(jnp.int32, (256, 256), 0)
    perm_from = lax.broadcasted_iota(jnp.int32, (256, 256), 1)
    swapped = (perm_to % 16) * 16 + perm_to // 16
    perm = jnp.where(perm_from == swapped, 1.0, 0.0).astype(BF16)

    def by_head(src, dst):
        for t in range(0, src.shape[0], 16):
            for h in range(0, heads, 16):
                tile = src[t : t + 16, h : h + 16, :].reshape(256, width)
                turned_tile = dot(perm, tile, NN).astype(BF16)
                dst[h : h + 16, t : t + 16, :] = turned_tile.reshape(16, 16, width)

    def scatter(src, dst_at, index):
        own = pltpu.make_async_copy(src.at[me], dst_at(me), recv_sem.at[index])
        own.start()

        def send(i, _):
            p = lax.rem(me + i, n)
            pltpu.make_async_remote_copy(
                src_ref=src.at[p], dst_ref=dst_at(me), send_sem=send_sem.at[index],
                recv_sem=recv_sem.at[index], device_id=(cand, p), device_id_type=MESH,
            ).start()
            return 0

        lax.fori_loop(1, n, send, 0)

    def received(whole, index):
        pltpu.make_async_copy(whole, whole, recv_sem.at[index]).wait()

    def sent(part, index):
        pltpu.make_async_copy(part, part, send_sem.at[index]).wait()

    loads[0].wait()
    by_head(ck_in, ck_out)
    loads[1].wait()
    by_head(cv_in, cv_out)
    pl.semaphore_wait(barrier, n)
    scatter(ck_out, lambda s: ck_all.at[half, s], 0)
    scatter(cv_out, lambda s: cv_all.at[half, s], 1)
    loads[2].wait()
    by_head(q_in, q_out)
    scatter(q_out, lambda s: q_all.at[s], 2)
    loads[3].wait()
    by_head(k_in, k_out)
    scatter(k_out, lambda s: k_all.at[s], 3)
    loads[4].wait()
    by_head(v_in, v_out)
    scatter(v_out, lambda s: v_all.at[s], 4)

    loads[5].wait()
    loads[6].wait()
    ext[1] = (hk[...].astype(F32) * hv[...].astype(F32)).astype(BF16)

    def halo(to):
        return pltpu.make_async_remote_copy(
            src_ref=ext.at[1], dst_ref=ext.at[0], send_sem=send_sem.at[5],
            recv_sem=recv_sem.at[5], device_id=(cand, to), device_id_type=MESH,
        )

    @pl.when(me + 1 < n)
    def _():
        halo(me + 1).start()

    loads[8].wait()

    taps = filt_ref.shape[0]
    turn_s = lax.broadcasted_iota(jnp.int32, (taps, taps), 0)
    turn_w = lax.broadcasted_iota(jnp.int32, (taps, taps), 1)
    turned = jnp.where((turn_s + turn_w) % taps == 0, 1.0, 0.0).astype(BF16)
    ring[...] = dot(filt_ref[...].astype(BF16), turned, TN)

    received(ck_all.at[half], 0)
    received(cv_all.at[half], 1)
    swaps = []
    for index, ref in ((6, ck_all), (7, cv_all)):
        swap = pltpu.make_async_remote_copy(
            src_ref=ref.at[half], dst_ref=ref.at[half], send_sem=send_sem.at[index],
            recv_sem=recv_sem.at[index], device_id=(partner, me), device_id_type=MESH,
        )
        swap.start()
        swaps.append(swap)
    for swap in swaps:
        swap.wait_recv()
    received(q_all, 2)

    def fold(state, query_block, key_rows, value_rows, mask=None):
        m, l, acc = state
        s = dot(query_block, key_rows, NT)
        if mask is not None:
            s = jnp.where(mask, s, LOW)
        top = jnp.maximum(m, jnp.max(s, axis=1, keepdims=True))
        w = jnp.exp2((s - top) * scale)
        shrink = jnp.exp2((m - top) * scale)
        l = l * shrink + jnp.sum(w, axis=1, keepdims=True)
        acc = acc * shrink + dot(w.astype(BF16), value_rows, NN)
        return top, l, acc

    block = min(512, length_all)
    per_block = block // rows
    blocks = length_all // block
    ctx_total = 2 * n * half_rows
    ctx_step = 1024 if ctx_total % 1024 == 0 else ctx_total
    q_flat = q_all.reshape(length_all, width)
    k_flat = k_all.reshape(length_all, width)
    v_flat = v_all.reshape(length_all, width)
    ck_flat = ck_all.reshape(ctx_total, width)
    cv_flat = cv_all.reshape(ctx_total, width)

    def over_context(i, _):
        at = pl.ds(pl.multiple_of(i * block, block), block)
        query_block = q_flat[at, :]
        state = (
            jnp.full((block, 1), LOW, F32), jnp.zeros((block, 1), F32), jnp.zeros((block, width), F32)
        )
        for j in range(ctx_total // ctx_step):
            part = slice(j * ctx_step, (j + 1) * ctx_step)
            state = fold(state, query_block, ck_flat[part, :], cv_flat[part, :])
        m_s[at, :], l_s[at, :], acc_s[at, :] = state
        return 0

    lax.fori_loop(0, blocks, over_context, 0)

    received(k_all, 3)
    received(v_all, 4)

    o_flat = o_out.reshape(length_all, width)
    own_step = 2 * block
    ahead = lax.broadcasted_iota(jnp.int32, (block, own_step), 1) - lax.broadcasted_iota(
        jnp.int32, (block, own_step), 0
    )

    def over_own(index, full):
        at = pl.ds(pl.multiple_of(index * block, block), block)
        query_block = q_flat[at, :]
        state = (m_s[at, :], l_s[at, :], acc_s[at, :])
        for t in range(full + 1):
            part = slice(t * own_step, (t + 1) * own_step)
            mask = ahead <= index * block - full * own_step if t == full else None
            state = fold(state, query_block, k_flat[part, :], v_flat[part, :], mask)
        o_flat[at, :] = (state[2] / state[1]).astype(BF16)

    def over_pair(step, _):
        low = lax.rem(step + me, blocks // 2)
        high = blocks - 1 - low
        for g in range(blocks // 4):

            @pl.when(low // 2 == g)
            def _():
                over_own(low, g)
                over_own(high, blocks // 2 - 1 - g)

        for index in (low, high):
            for r in range(per_block):
                p = index * per_block + r

                @pl.when(p != me)
                def _():
                    pltpu.make_async_remote_copy(
                        src_ref=o_out.at[p], dst_ref=o_in.at[me], send_sem=send_sem.at[8],
                        recv_sem=recv_sem.at[8], device_id=(cand, p), device_id_type=MESH,
                    ).start()
        return 0

    lax.fori_loop(0, blocks // 2, over_pair, 0)
    pltpu.make_async_copy(o_out.at[me], o_in.at[me], recv_sem.at[8]).start()

    @pl.when(me == 0)
    def _():
        def shift(j, _):
            cols = pl.ds(pl.multiple_of(j * 512, 512), 512)
            held = tail[:, cols].astype(F32)
            ext[0, :, cols] = jnp.concatenate([jnp.zeros((1, 512), F32), held], axis=0).astype(BF16)
            return 0

        lax.fori_loop(0, tail.shape[1] // 512, shift, 0)

    @pl.when(me > 0)
    def _():
        halo(me).wait_recv()

    loads[7].wait()
    valid = len_ref[0] - me * rows
    out_row = lax.broadcasted_iota(jnp.int32, (rows, 128), 0)
    out_col = lax.broadcasted_iota(jnp.int32, (rows, 128), 1)
    keep = out_row < valid
    before = out_col > out_row
    lane_group = out_col // (128 // groups_per_tile)

    def filtered(j, _):
        cols = pl.ds(pl.multiple_of(j * 128, 128), 128)
        eight = ring[pl.ds(pl.multiple_of(j * groups_per_tile, groups_per_tile), groups_per_tile), :]
        earlier = []
        current = []
        for g in range(groups_per_tile):
            spread = jnp.broadcast_to(eight[g : g + 1, :], (rows, 128))
            turns = pltpu.roll(spread, 0, 1, stride=1, stride_axis=0)
            earlier.append(jnp.where(before, turns, 0.0).astype(BF16))
            current.append(jnp.where(before, 0.0, turns).astype(BF16))
        mats = jnp.concatenate(
            [jnp.concatenate(earlier, axis=0), jnp.concatenate(current, axis=0)], axis=1
        )
        stream = jnp.concatenate([ext[0, :, cols], ext[1, :, cols]], axis=0)
        every = dot(mats, stream, NN)
        mixed = every[:rows]
        for g in range(1, groups_per_tile):
            mixed = jnp.where(lane_group == g, every[g * rows : (g + 1) * rows], mixed)
        gated = jnp.where(keep, hq[:, cols].astype(F32) * mixed, 0.0)
        hy_ref[0, :, cols] = gated.astype(BF16)
        return 0

    lax.fori_loop(0, ext.shape[2] // 128, filtered, 0, unroll=2)

    received(o_in, 8)
    row_of = lax.broadcasted_iota(jnp.int32, (256, width), 0) // 16
    for t in range(0, rows, 16):
        for h in range(0, heads, 16):
            tile = o_in[h : h + 16, t : t + 16, :].reshape(256, width)
            kept = jnp.where(row_of < valid - t, dot(perm, tile, NN), 0.0).astype(BF16)
            att_ref[0, t : t + 16, h : h + 16, :] = kept.reshape(16, 16, width)

    for index, ref in ((0, ck_out), (1, cv_out), (2, q_out), (3, k_out), (4, v_out), (8, o_out)):
        sent(ref.at[pl.ds(0, n - 1)], index)

    @pl.when(me + 1 < n)
    def _():
        halo(me + 1).wait_send()

    for swap in swaps:
        swap.wait_send()


def local(
    hyena_query, hyena_key, hyena_value, hyena_filters, context_tail,
    cont_queries, cont_keys, cont_values, context_keys, context_values, lengths,
):
    n = lax.axis_size("seq")
    _, rows, channels = hyena_key.shape
    heads, width = cont_queries.shape[2:]
    half_rows = context_keys.shape[0] // 2
    taps, groups = hyena_filters.shape
    groups_per_tile = 128 * groups // channels
    length_all = n * rows
    scale = math.log2(math.e) / math.sqrt(width)
    hbm = pl.BlockSpec(memory_space=pl.ANY)
    vmem = pl.BlockSpec(memory_space=pltpu.VMEM)
    block = pltpu.VMEM((rows, heads, width), BF16)
    per_head = pltpu.VMEM((n, rows, width), BF16)
    half_block = pltpu.VMEM((half_rows, heads, width), BF16)
    half_heads = pltpu.VMEM((n, half_rows, width), BF16)
    both_halves = pltpu.VMEM((2, n, half_rows, width), BF16)
    stream = pltpu.VMEM((rows, channels), BF16)
    return pl.pallas_call(
        functools.partial(fused, n, groups_per_tile, scale),
        out_shape=(
            jax.ShapeDtypeStruct(hyena_query.shape, BF16),
            jax.ShapeDtypeStruct(cont_queries.shape, BF16),
        ),
        in_specs=[hbm, hbm, hbm, vmem, hbm, hbm, hbm, hbm, hbm, hbm,
                  pl.BlockSpec(memory_space=pltpu.SMEM)],
        out_specs=(vmem, vmem),
        scratch_shapes=[
            stream, stream, stream,
            pltpu.VMEM(context_tail.shape, BF16),
            pltpu.VMEM((2, rows, channels), BF16),
            pltpu.VMEM((groups, taps), F32),
            block, block, block, half_block, half_block,
            per_head, per_head, per_head, half_heads, half_heads,
            per_head, per_head, per_head, both_halves, both_halves,
            pltpu.VMEM((length_all, 1), F32), pltpu.VMEM((length_all, 1), F32),
            pltpu.VMEM((length_all, width), F32),
            per_head, per_head,
            pltpu.SemaphoreType.DMA((9,)), pltpu.SemaphoreType.DMA((9,)), pltpu.SemaphoreType.DMA((9,)),
        ],
        compiler_params=pltpu.CompilerParams(
            collective_id=0, has_side_effects=True, vmem_limit_bytes=63 * 2**20
        ),
        name="fused",
    )(
        hyena_query, hyena_key, hyena_value, hyena_filters, context_tail,
        cont_queries, cont_keys, cont_values, context_keys, context_values, lengths,
    )


def solution(mesh):
    placed = (
        P("cand", "seq", None), P("cand", "seq", None), P("cand", "seq", None), P(), P(),
        P("cand", "seq", None, None), P("cand", "seq", None, None), P("cand", "seq", None, None),
        P("seq", None, None), P("seq", None, None), P("cand"),
    )
    return jax.shard_map(
        local, mesh=mesh, in_specs=placed,
        out_specs=(P("cand", "seq", None), P("cand", "seq", None, None)), check_vma=False,
    )
```

```python
import functools
import math

import jax
import jax.numpy as jnp
from jax import lax
from jax.experimental import pallas as pl
from jax.experimental.pallas import tpu as pltpu
from jax.sharding import PartitionSpec as P

F32 = jnp.float32
BF16 = jnp.bfloat16
MESH = pl.DeviceIdType.MESH
NT = (((1,), (1,)), ((), ()))
NN = (((1,), (0,)), ((), ()))
TN = (((0,), (0,)), ((), ()))
LOW = -1e30
RING = 4


def dot(a, b, dims):
    return lax.dot_general(a, b, dims, preferred_element_type=F32)


def leading_swap():
    to = lax.broadcasted_iota(jnp.int32, (256, 256), 0)
    source = lax.broadcasted_iota(jnp.int32, (256, 256), 1)
    return jnp.where(source == (to % 16) * 16 + to // 16, 1.0, 0.0).astype(BF16)


def finish(hy_ref, o_ref, len_ref, hy_out, att_ref):
    heads, rows, width = o_ref.shape
    total_rows = pl.num_programs(0) * rows
    start = lax.axis_index("seq") * total_rows + pl.program_id(0) * rows
    valid = len_ref[0] - start
    perm = leading_swap()
    row_of = lax.broadcasted_iota(jnp.int32, (256, width), 0) // 16
    for t in range(0, rows, 16):
        for h in range(0, heads, 16):
            tile = o_ref[h : h + 16, t : t + 16, :].reshape(256, width)
            kept = jnp.where(row_of < valid - t, dot(perm, tile, NN), 0.0).astype(BF16)
            att_ref[0, t : t + 16, h : h + 16, :] = kept.reshape(16, 16, width)
    hy_out[...] = hy_ref[...]


def fused(
    n, groups_per_tile, scale,
    hq_hbm, hk_hbm, hv_hbm, filt_ref, tail_hbm, q_hbm, k_hbm, v_hbm, ck_hbm, cv_hbm, len_ref,
    hy_ref, o_in,
    hq, hk, hv, tail, ext, ring, mats,
    q_in, k_in, v_in, ck_in, cv_in,
    q_out, k_out, v_out, ck_out, cv_out,
    q_all, k_all, v_all, ck_all, cv_all,
    m_s, l_s, acc_s, o_out,
    load_sem, send_sem, recv_sem,
):
    rows, heads, width = q_in.shape
    half_rows = ck_in.shape[0]
    length_all = n * rows
    me = lax.axis_index("seq")
    cand = lax.axis_index("cand")
    half = lax.rem(cand, 2)
    partner = cand + 1 - 2 * half

    barrier = pltpu.get_barrier_semaphore()

    def greet(i, _):
        pl.semaphore_signal(
            barrier, inc=1, device_id=(cand, lax.rem(me + i, n)), device_id_type=MESH
        )
        return 0

    lax.fori_loop(1, n, greet, 0)
    pl.semaphore_signal(barrier, inc=1, device_id=(partner, me), device_id_type=MESH)

    ctx_rows = pl.ds(half * half_rows, half_rows)
    loads = [
        pltpu.make_async_copy(ck_hbm.at[ctx_rows], ck_in, load_sem.at[0]),
        pltpu.make_async_copy(cv_hbm.at[ctx_rows], cv_in, load_sem.at[1]),
        pltpu.make_async_copy(q_hbm.at[0], q_in, load_sem.at[2]),
        pltpu.make_async_copy(k_hbm.at[0], k_in, load_sem.at[3]),
        pltpu.make_async_copy(v_hbm.at[0], v_in, load_sem.at[4]),
        pltpu.make_async_copy(hk_hbm.at[0], hk, load_sem.at[5]),
        pltpu.make_async_copy(hv_hbm.at[0], hv, load_sem.at[6]),
        pltpu.make_async_copy(hq_hbm.at[0], hq, load_sem.at[7]),
        pltpu.make_async_copy(tail_hbm, tail, load_sem.at[8]),
    ]
    for copy in loads:
        copy.start()

    perm = leading_swap()

    def by_head(src, dst):
        for t in range(0, src.shape[0], 16):
            for h in range(0, heads, 16):
                tile = src[t : t + 16, h : h + 16, :].reshape(256, width)
                turned_tile = dot(perm, tile, NN).astype(BF16)
                dst[h : h + 16, t : t + 16, :] = turned_tile.reshape(16, 16, width)

    column = me - lax.rem(me, RING)

    def scatter(src, dst_at, index):
        own = pltpu.make_async_copy(src.at[me], dst_at(me), recv_sem.at[index])
        own.start()

        def send(i):
            p = lax.rem(me + i, n)
            pltpu.make_async_remote_copy(
                src_ref=src.at[p], dst_ref=dst_at(me), send_sem=send_sem.at[index],
                recv_sem=recv_sem.at[index], device_id=(cand, p), device_id_type=MESH,
            ).start()

        lax.fori_loop(1, n, lambda i, _: (send(i), 0)[1], 0)

    def received(whole, index):
        pltpu.make_async_copy(whole, whole, recv_sem.at[index]).wait()

    def sent(part, index):
        pltpu.make_async_copy(part, part, send_sem.at[index]).wait()

    loads[2].wait()
    by_head(q_in, q_out)
    loads[0].wait()
    by_head(ck_in, ck_out)
    loads[1].wait()
    by_head(cv_in, cv_out)
    pl.semaphore_wait(barrier, n)
    scatter(ck_out, lambda s: ck_all.at[half, s], 0)
    scatter(cv_out, lambda s: cv_all.at[half, s], 1)
    scatter(q_out, lambda s: q_all.at[s], 2)
    loads[3].wait()
    by_head(k_in, k_out)
    scatter(k_out, lambda s: k_all.at[s], 3)
    loads[4].wait()
    by_head(v_in, v_out)
    scatter(v_out, lambda s: v_all.at[s], 4)

    loads[5].wait()
    loads[6].wait()
    ext[1] = (hk[...].astype(F32) * hv[...].astype(F32)).astype(BF16)

    def halo(to, piece):
        part = pl.ds(piece * 16, 16)
        return pltpu.make_async_remote_copy(
            src_ref=ext.at[1, part], dst_ref=ext.at[0, part], send_sem=send_sem.at[5],
            recv_sem=recv_sem.at[5], device_id=(cand, to), device_id_type=MESH,
        )

    @pl.when(me + 1 < n)
    def _():
        for piece in range(rows // 16):
            halo(me + 1, piece).start()

    loads[8].wait()

    taps = filt_ref.shape[0]
    turn_s = lax.broadcasted_iota(jnp.int32, (taps, taps), 0)
    turn_w = lax.broadcasted_iota(jnp.int32, (taps, taps), 1)
    turned = jnp.where((turn_s + turn_w) % taps == 0, 1.0, 0.0).astype(BF16)
    ring[...] = dot(filt_ref[...].astype(BF16), turned, TN)


    tiles = ext.shape[2] // 128
    out_row = lax.broadcasted_iota(jnp.int32, (rows, 128), 0)
    out_col = lax.broadcasted_iota(jnp.int32, (rows, 128), 1)
    before = out_col > out_row

    def filter_matrices(j, _):
        some = ring[pl.ds(pl.multiple_of(j * groups_per_tile, groups_per_tile), groups_per_tile), :]
        for g in range(groups_per_tile):
            line = jnp.broadcast_to(some[g : g + 1, :], (rows, 128))
            turns = pltpu.roll(line, 0, 1, stride=1, stride_axis=0)
            part = slice(g * rows, (g + 1) * rows)
            mats[j, part, :128] = jnp.where(before, turns, 0.0).astype(BF16)
            mats[j, part, 128:] = jnp.where(before, 0.0, turns).astype(BF16)
        return 0

    lax.fori_loop(0, tiles, filter_matrices, 0, unroll=2)

    received(ck_all.at[half], 0)
    received(cv_all.at[half], 1)
    swaps = []
    for index, ref in ((6, ck_all), (7, cv_all)):
        swap = pltpu.make_async_remote_copy(
            src_ref=ref.at[half], dst_ref=ref.at[half], send_sem=send_sem.at[index],
            recv_sem=recv_sem.at[index], device_id=(partner, me), device_id_type=MESH,
        )
        swap.start()
        swaps.append(swap)
    for swap in swaps:
        swap.wait_recv()
    received(q_all, 2)

    def spread(column):
        return jnp.broadcast_to(column, (column.shape[0], width))

    def fold(state, query_block, key_rows, value_rows, mask=None):
        m, l, acc = state
        s = dot(query_block, key_rows, NT)
        if mask is not None:
            s = jnp.where(mask, s, LOW)
        top = jnp.maximum(m, spread(jnp.max(s, axis=1, keepdims=True)))
        w = jnp.exp2((s - jnp.concatenate([top] * (s.shape[1] // width), axis=1)) * scale)
        shrink = jnp.exp2((m - top) * scale)
        l = l * shrink + spread(jnp.sum(w, axis=1, keepdims=True))
        acc = acc * shrink + dot(w.astype(BF16), value_rows, NN)
        return top, l, acc

    block = min(512, length_all)
    per_block = block // rows
    blocks = length_all // block
    ctx_total = 2 * n * half_rows
    ctx_step = 1024 if ctx_total % 1024 == 0 else ctx_total
    q_flat = q_all.reshape(length_all, width)
    k_flat = k_all.reshape(length_all, width)
    v_flat = v_all.reshape(length_all, width)
    ck_flat = ck_all.reshape(ctx_total, width)
    cv_flat = cv_all.reshape(ctx_total, width)

    def over_context(i, _):
        at = pl.ds(pl.multiple_of(i * block, block), block)
        query_block = q_flat[at, :]
        state = (
            jnp.full((block, width), LOW, F32), jnp.zeros((block, width), F32),
            jnp.zeros((block, width), F32),
        )
        for j in range(ctx_total // ctx_step):
            part = slice(j * ctx_step, (j + 1) * ctx_step)
            state = fold(state, query_block, ck_flat[part, :], cv_flat[part, :])
        m_s[at, :], l_s[at, :], acc_s[at, :] = state
        return 0

    lax.fori_loop(0, blocks, over_context, 0)

    received(k_all, 3)
    received(v_all, 4)

    o_flat = o_out.reshape(length_all, width)
    own_step = 2 * block
    ahead = lax.broadcasted_iota(jnp.int32, (block, own_step), 1) - lax.broadcasted_iota(
        jnp.int32, (block, own_step), 0
    )

    def over_own(index, full):
        at = pl.ds(pl.multiple_of(index * block, block), block)
        query_block = q_flat[at, :]
        state = (m_s[at, :], l_s[at, :], acc_s[at, :])
        for t in range(full + 1):
            part = slice(t * own_step, (t + 1) * own_step)
            mask = ahead <= index * block - full * own_step if t == full else None
            state = fold(state, query_block, k_flat[part, :], v_flat[part, :], mask)
        o_flat[at, :] = (state[2] / state[1]).astype(BF16)

    def over_pair(step, _):
        low = lax.rem(step + column // RING, blocks // 2)
        high = blocks - 1 - low
        for g in range(blocks // 4):

            @pl.when(low // 2 == g)
            def _():
                over_own(low, g)
                over_own(high, blocks // 2 - 1 - g)

        for index in (low, high):
            for r in range(per_block):
                p = index * per_block + r

                @pl.when(p != me)
                def _():
                    pltpu.make_async_remote_copy(
                        src_ref=o_out.at[p], dst_ref=o_in.at[me], send_sem=send_sem.at[8],
                        recv_sem=recv_sem.at[8], device_id=(cand, p), device_id_type=MESH,
                    ).start()
        return 0

    lax.fori_loop(0, blocks // 2, over_pair, 0)
    pltpu.make_async_copy(o_out.at[me], o_in.at[me], recv_sem.at[8]).start()

    @pl.when(me == 0)
    def _():
        def shift(j, _):
            cols = pl.ds(pl.multiple_of(j * 512, 512), 512)
            held = tail[:, cols].astype(F32)
            ext[0, :, cols] = jnp.concatenate([jnp.zeros((1, 512), F32), held], axis=0).astype(BF16)
            return 0

        lax.fori_loop(0, tail.shape[1] // 512, shift, 0)

    @pl.when(me > 0)
    def _():
        received(ext.at[0], 5)

    loads[7].wait()
    valid = len_ref[0] - me * rows
    keep = out_row < valid
    lane_group = out_col // (128 // groups_per_tile)

    def filtered(j, _):
        cols = pl.ds(pl.multiple_of(j * 128, 128), 128)
        stream = jnp.concatenate([ext[0, :, cols], ext[1, :, cols]], axis=0)
        every = dot(mats[j], stream, NN)
        mixed = every[:rows]
        for g in range(1, groups_per_tile):
            mixed = jnp.where(lane_group == g, every[g * rows : (g + 1) * rows], mixed)
        gated = jnp.where(keep, hq[:, cols].astype(F32) * mixed, 0.0)
        hy_ref[0, :, cols] = gated.astype(BF16)
        return 0

    lax.fori_loop(0, tiles, filtered, 0, unroll=4)

    received(o_in, 8)
    for index, ref in ((0, ck_out), (1, cv_out), (4, v_out), (8, o_out)):
        sent(ref.at[pl.ds(0, n - 1)], index)
    for index, ref in ((2, q_out), (3, k_out)):
        sent(ref.at[pl.ds(0, n - 1)], index)

    @pl.when(me + 1 < n)
    def _():
        sent(ext.at[1], 5)

    for swap in swaps:
        swap.wait_send()


def local(
    hyena_query, hyena_key, hyena_value, hyena_filters, context_tail,
    cont_queries, cont_keys, cont_values, context_keys, context_values, lengths,
):
    n = lax.axis_size("seq")
    _, rows, channels = hyena_key.shape
    heads, width = cont_queries.shape[2:]
    half_rows = context_keys.shape[0] // 2
    taps, groups = hyena_filters.shape
    groups_per_tile = 128 * groups // channels
    length_all = n * rows
    scale = math.log2(math.e) / math.sqrt(width)
    hbm = pl.BlockSpec(memory_space=pl.ANY)
    vmem = pl.BlockSpec(memory_space=pltpu.VMEM)
    block = pltpu.VMEM((rows, heads, width), BF16)
    per_head = pltpu.VMEM((n, rows, width), BF16)
    half_block = pltpu.VMEM((half_rows, heads, width), BF16)
    half_heads = pltpu.VMEM((n, half_rows, width), BF16)
    both_halves = pltpu.VMEM((2, n, half_rows, width), BF16)
    stream = pltpu.VMEM((rows, channels), BF16)
    hyena, by_heads = pl.pallas_call(
        functools.partial(fused, n, groups_per_tile, scale),
        out_shape=(
            jax.ShapeDtypeStruct(hyena_query.shape, BF16),
            jax.ShapeDtypeStruct((n, rows, width), BF16),
        ),
        in_specs=[hbm, hbm, hbm, vmem, hbm, hbm, hbm, hbm, hbm, hbm,
                  pl.BlockSpec(memory_space=pltpu.SMEM)],
        out_specs=(vmem, vmem),
        scratch_shapes=[
            stream, stream, stream,
            pltpu.VMEM(context_tail.shape, BF16),
            pltpu.VMEM((2, rows, channels), BF16),
            pltpu.VMEM((groups, taps), F32),
            pltpu.VMEM((channels // 128, groups_per_tile * rows, 2 * rows), BF16),
            block, block, block, half_block, half_block,
            per_head, per_head, per_head, half_heads, half_heads,
            per_head, per_head, per_head, both_halves, both_halves,
            pltpu.VMEM((length_all, width), F32), pltpu.VMEM((length_all, width), F32),
            pltpu.VMEM((length_all, width), F32),
            per_head,
            pltpu.SemaphoreType.DMA((9,)), pltpu.SemaphoreType.DMA((9,)), pltpu.SemaphoreType.DMA((9,)),
        ],
        compiler_params=pltpu.CompilerParams(
            collective_id=0, has_side_effects=True, vmem_limit_bytes=63 * 2**20
        ),
        name="fused",
    )(
        hyena_query, hyena_key, hyena_value, hyena_filters, context_tail,
        cont_queries, cont_keys, cont_values, context_keys, context_values, lengths,
    )
    part = rows // 2
    hy_spec = pl.BlockSpec((1, part, channels), lambda i: (0, i, 0))
    return pl.pallas_call(
        finish,
        grid=(rows // part,),
        out_shape=(
            jax.ShapeDtypeStruct(hyena_query.shape, BF16),
            jax.ShapeDtypeStruct(cont_queries.shape, BF16),
        ),
        in_specs=[hy_spec, pl.BlockSpec((n, part, width), lambda i: (0, i, 0)),
                  pl.BlockSpec(memory_space=pltpu.SMEM)],
        out_specs=(hy_spec, pl.BlockSpec((1, part, heads, width), lambda i: (0, i, 0, 0))),
        name="finish",
    )(hyena, by_heads, lengths)


def solution(mesh):
    placed = (
        P("cand", "seq", None), P("cand", "seq", None), P("cand", "seq", None), P(), P(),
        P("cand", "seq", None, None), P("cand", "seq", None, None), P("cand", "seq", None, None),
        P("seq", None, None), P("seq", None, None), P("cand"),
    )
    return jax.shard_map(
        local, mesh=mesh, in_specs=placed,
        out_specs=(P("cand", "seq", None), P("cand", "seq", None, None)), check_vma=False,
    )
```

```python
import functools
import math

import jax
import jax.numpy as jnp
from jax import lax
from jax.experimental import pallas as pl
from jax.experimental.pallas import tpu as pltpu
from jax.sharding import PartitionSpec as P

F32 = jnp.float32
BF16 = jnp.bfloat16
MESH = pl.DeviceIdType.MESH
NT = (((1,), (1,)), ((), ()))
NN = (((1,), (0,)), ((), ()))
TN = (((0,), (0,)), ((), ()))
LOW = -1e30
RING = 4


def dot(a, b, dims):
    return lax.dot_general(a, b, dims, preferred_element_type=F32)


def leading_swap():
    to = lax.broadcasted_iota(jnp.int32, (256, 256), 0)
    source = lax.broadcasted_iota(jnp.int32, (256, 256), 1)
    return jnp.where(source == (to % 16) * 16 + to // 16, 1.0, 0.0).astype(BF16)


def finish(hy_ref, o_ref, len_ref, hy_out, att_ref):
    heads, rows, width = o_ref.shape
    total_rows = pl.num_programs(0) * rows
    start = lax.axis_index("seq") * total_rows + pl.program_id(0) * rows
    valid = len_ref[0] - start
    perm = leading_swap()
    row_of = lax.broadcasted_iota(jnp.int32, (256, width), 0) // 16
    for t in range(0, rows, 16):
        for h in range(0, heads, 16):
            tile = o_ref[h : h + 16, t : t + 16, :].reshape(256, width)
            kept = jnp.where(row_of < valid - t, dot(perm, tile, NN), 0.0).astype(BF16)
            att_ref[0, t : t + 16, h : h + 16, :] = kept.reshape(16, 16, width)
    hy_out[...] = hy_ref[...]


def fused(
    n, groups_per_tile, scale,
    hq_hbm, hk_hbm, hv_hbm, filt_ref, tail_hbm, q_hbm, k_hbm, v_hbm, ck_hbm, cv_hbm, len_ref,
    hy_hbm, o_in,
    hq, hk, hv, hy, tail, ext, ring, mats,
    q_in, k_in, v_in, ck_in, cv_in,
    q_out, k_out, v_out, ck_out, cv_out,
    q_all, k_all, v_all, ck_all, cv_all,
    m_s, l_s, acc_s, o_out,
    load_sem, send_sem, recv_sem,
):
    rows, heads, width = q_in.shape
    half_rows = ck_in.shape[0]
    length_all = n * rows
    me = lax.axis_index("seq")
    cand = lax.axis_index("cand")
    half = lax.rem(cand, 2)
    partner = cand + 1 - 2 * half

    barrier = pltpu.get_barrier_semaphore()

    def greet(i, _):
        pl.semaphore_signal(
            barrier, inc=1, device_id=(cand, lax.rem(me + i, n)), device_id_type=MESH
        )
        return 0

    lax.fori_loop(1, n, greet, 0)
    pl.semaphore_signal(barrier, inc=1, device_id=(partner, me), device_id_type=MESH)

    ctx_rows = pl.ds(half * half_rows, half_rows)
    loads = [
        pltpu.make_async_copy(ck_hbm.at[ctx_rows], ck_in, load_sem.at[0]),
        pltpu.make_async_copy(cv_hbm.at[ctx_rows], cv_in, load_sem.at[1]),
        pltpu.make_async_copy(q_hbm.at[0], q_in, load_sem.at[2]),
        pltpu.make_async_copy(k_hbm.at[0], k_in, load_sem.at[3]),
        pltpu.make_async_copy(v_hbm.at[0], v_in, load_sem.at[4]),
        pltpu.make_async_copy(hk_hbm.at[0], hk, load_sem.at[5]),
        pltpu.make_async_copy(hv_hbm.at[0], hv, load_sem.at[6]),
        pltpu.make_async_copy(hq_hbm.at[0], hq, load_sem.at[7]),
        pltpu.make_async_copy(tail_hbm, tail, load_sem.at[8]),
    ]
    for copy in loads:
        copy.start()

    perm = leading_swap()

    def by_head(src, dst):
        for t in range(0, src.shape[0], 16):
            for h in range(0, heads, 16):
                tile = src[t : t + 16, h : h + 16, :].reshape(256, width)
                turned_tile = dot(perm, tile, NN).astype(BF16)
                dst[h : h + 16, t : t + 16, :] = turned_tile.reshape(16, 16, width)

    column = me - lax.rem(me, RING)

    def scatter(src, dst_at, index):
        own = pltpu.make_async_copy(src.at[me], dst_at(me), recv_sem.at[index])
        own.start()

        def send(i):
            p = lax.rem(me + i, n)
            pltpu.make_async_remote_copy(
                src_ref=src.at[p], dst_ref=dst_at(me), send_sem=send_sem.at[index],
                recv_sem=recv_sem.at[index], device_id=(cand, p), device_id_type=MESH,
            ).start()

        lax.fori_loop(1, n, lambda i, _: (send(i), 0)[1], 0)

    def received(whole, index):
        pltpu.make_async_copy(whole, whole, recv_sem.at[index]).wait()

    def sent(part, index):
        pltpu.make_async_copy(part, part, send_sem.at[index]).wait()

    loads[0].wait()
    by_head(ck_in, ck_out)
    loads[1].wait()
    by_head(cv_in, cv_out)
    pl.semaphore_wait(barrier, n)
    scatter(ck_out, lambda s: ck_all.at[half, s], 0)
    scatter(cv_out, lambda s: cv_all.at[half, s], 1)
    loads[2].wait()
    by_head(q_in, q_out)
    scatter(q_out, lambda s: q_all.at[s], 2)
    loads[3].wait()
    by_head(k_in, k_out)
    scatter(k_out, lambda s: k_all.at[s], 3)
    loads[4].wait()
    by_head(v_in, v_out)
    scatter(v_out, lambda s: v_all.at[s], 4)

    loads[5].wait()
    loads[6].wait()
    ext[1] = (hk[...].astype(F32) * hv[...].astype(F32)).astype(BF16)

    def halo(to, piece):
        part = pl.ds(piece * 16, 16)
        return pltpu.make_async_remote_copy(
            src_ref=ext.at[1, part], dst_ref=ext.at[0, part], send_sem=send_sem.at[5],
            recv_sem=recv_sem.at[5], device_id=(cand, to), device_id_type=MESH,
        )

    @pl.when(me + 1 < n)
    def _():
        for piece in range(rows // 16):
            halo(me + 1, piece).start()

    loads[8].wait()

    taps = filt_ref.shape[0]
    turn_s = lax.broadcasted_iota(jnp.int32, (taps, taps), 0)
    turn_w = lax.broadcasted_iota(jnp.int32, (taps, taps), 1)
    turned = jnp.where((turn_s + turn_w) % taps == 0, 1.0, 0.0).astype(BF16)
    ring[...] = dot(filt_ref[...].astype(BF16), turned, TN)


    tiles = ext.shape[2] // 128
    out_row = lax.broadcasted_iota(jnp.int32, (rows, 128), 0)
    out_col = lax.broadcasted_iota(jnp.int32, (rows, 128), 1)
    before = out_col > out_row

    def filter_matrices(j, _):
        some = ring[pl.ds(pl.multiple_of(j * groups_per_tile, groups_per_tile), groups_per_tile), :]
        for g in range(groups_per_tile):
            line = jnp.broadcast_to(some[g : g + 1, :], (rows, 128))
            turns = pltpu.roll(line, 0, 1, stride=1, stride_axis=0)
            part = slice(g * rows, (g + 1) * rows)
            mats[j, part, :128] = jnp.where(before, turns, 0.0).astype(BF16)
            mats[j, part, 128:] = jnp.where(before, 0.0, turns).astype(BF16)
        return 0

    lax.fori_loop(0, tiles, filter_matrices, 0, unroll=2)

    received(ck_all.at[half], 0)
    received(cv_all.at[half], 1)
    swaps = []
    for index, ref in ((6, ck_all), (7, cv_all)):
        swap = pltpu.make_async_remote_copy(
            src_ref=ref.at[half], dst_ref=ref.at[half], send_sem=send_sem.at[index],
            recv_sem=recv_sem.at[index], device_id=(partner, me), device_id_type=MESH,
        )
        swap.start()
        swaps.append(swap)
    for swap in swaps:
        swap.wait_recv()
    received(q_all, 2)

    def spread(column):
        return jnp.broadcast_to(column, (column.shape[0], width))

    def fold(state, query_block, key_rows, value_rows, mask=None):
        m, l, acc = state
        s = dot(query_block, key_rows, NT)
        if mask is not None:
            s = jnp.where(mask, s, LOW)
        top = jnp.maximum(m, spread(jnp.max(s, axis=1, keepdims=True)))
        w = jnp.exp2((s - jnp.concatenate([top] * (s.shape[1] // width), axis=1)) * scale)
        shrink = jnp.exp2((m - top) * scale)
        l = l * shrink + spread(jnp.sum(w, axis=1, keepdims=True))
        acc = acc * shrink + dot(w.astype(BF16), value_rows, NN)
        return top, l, acc

    block = min(512, length_all)
    per_block = block // rows
    blocks = length_all // block
    ctx_total = 2 * n * half_rows
    ctx_step = 1024 if ctx_total % 1024 == 0 else ctx_total
    q_flat = q_all.reshape(length_all, width)
    k_flat = k_all.reshape(length_all, width)
    v_flat = v_all.reshape(length_all, width)
    ck_flat = ck_all.reshape(ctx_total, width)
    cv_flat = cv_all.reshape(ctx_total, width)

    def over_context(i, _):
        at = pl.ds(pl.multiple_of(i * block, block), block)
        query_block = q_flat[at, :]
        state = (
            jnp.full((block, width), LOW, F32), jnp.zeros((block, width), F32),
            jnp.zeros((block, width), F32),
        )
        for j in range(ctx_total // ctx_step):
            part = slice(j * ctx_step, (j + 1) * ctx_step)
            state = fold(state, query_block, ck_flat[part, :], cv_flat[part, :])
        m_s[at, :], l_s[at, :], acc_s[at, :] = state
        return 0

    lax.fori_loop(0, blocks, over_context, 0)

    received(k_all, 3)
    received(v_all, 4)

    o_flat = o_out.reshape(length_all, width)
    own_step = 2 * block
    ahead = lax.broadcasted_iota(jnp.int32, (block, own_step), 1) - lax.broadcasted_iota(
        jnp.int32, (block, own_step), 0
    )

    def over_own(index, full):
        at = pl.ds(pl.multiple_of(index * block, block), block)
        query_block = q_flat[at, :]
        state = (m_s[at, :], l_s[at, :], acc_s[at, :])
        for t in range(full + 1):
            part = slice(t * own_step, (t + 1) * own_step)
            mask = ahead <= index * block - full * own_step if t == full else None
            state = fold(state, query_block, k_flat[part, :], v_flat[part, :], mask)
        o_flat[at, :] = (state[2] / state[1]).astype(BF16)

    def over_pair(step, _):
        low = lax.rem(step + column // RING, blocks // 2)
        high = blocks - 1 - low
        for g in range(blocks // 4):

            @pl.when(low // 2 == g)
            def _():
                over_own(low, g)
                over_own(high, blocks // 2 - 1 - g)

        for index in (low, high):
            for r in range(per_block):
                p = index * per_block + r

                @pl.when(p != me)
                def _():
                    pltpu.make_async_remote_copy(
                        src_ref=o_out.at[p], dst_ref=o_in.at[me], send_sem=send_sem.at[8],
                        recv_sem=recv_sem.at[8], device_id=(cand, p), device_id_type=MESH,
                    ).start()
        return 0

    lax.fori_loop(0, blocks // 2, over_pair, 0)
    pltpu.make_async_copy(o_out.at[me], o_in.at[me], recv_sem.at[8]).start()

    @pl.when(me == 0)
    def _():
        def shift(j, _):
            cols = pl.ds(pl.multiple_of(j * 512, 512), 512)
            held = tail[:, cols].astype(F32)
            ext[0, :, cols] = jnp.concatenate([jnp.zeros((1, 512), F32), held], axis=0).astype(BF16)
            return 0

        lax.fori_loop(0, tail.shape[1] // 512, shift, 0)

    @pl.when(me > 0)
    def _():
        received(ext.at[0], 5)

    loads[7].wait()
    valid = len_ref[0] - me * rows
    keep = out_row < valid
    lane_group = out_col // (128 // groups_per_tile)

    def filtered(j, _):
        cols = pl.ds(pl.multiple_of(j * 128, 128), 128)
        stream = jnp.concatenate([ext[0, :, cols], ext[1, :, cols]], axis=0)
        every = dot(mats[j], stream, NN)
        mixed = every[:rows]
        for g in range(1, groups_per_tile):
            mixed = jnp.where(lane_group == g, every[g * rows : (g + 1) * rows], mixed)
        gated = jnp.where(keep, hq[:, cols].astype(F32) * mixed, 0.0)
        hy[:, cols] = gated.astype(BF16)
        return 0

    lax.fori_loop(0, tiles, filtered, 0, unroll=4)

    store = pltpu.make_async_copy(hy, hy_hbm.at[0], load_sem.at[7])
    store.start()

    received(o_in, 8)
    store.wait()
    for index, ref in ((0, ck_out), (1, cv_out), (4, v_out), (8, o_out)):
        sent(ref.at[pl.ds(0, n - 1)], index)
    for index, ref in ((2, q_out), (3, k_out)):
        sent(ref.at[pl.ds(0, n - 1)], index)

    @pl.when(me + 1 < n)
    def _():
        sent(ext.at[1], 5)

    for swap in swaps:
        swap.wait_send()


def local(
    hyena_query, hyena_key, hyena_value, hyena_filters, context_tail,
    cont_queries, cont_keys, cont_values, context_keys, context_values, lengths,
):
    n = lax.axis_size("seq")
    _, rows, channels = hyena_key.shape
    heads, width = cont_queries.shape[2:]
    half_rows = context_keys.shape[0] // 2
    taps, groups = hyena_filters.shape
    groups_per_tile = 128 * groups // channels
    length_all = n * rows
    scale = math.log2(math.e) / math.sqrt(width)
    hbm = pl.BlockSpec(memory_space=pl.ANY)
    vmem = pl.BlockSpec(memory_space=pltpu.VMEM)
    block = pltpu.VMEM((rows, heads, width), BF16)
    per_head = pltpu.VMEM((n, rows, width), BF16)
    half_block = pltpu.VMEM((half_rows, heads, width), BF16)
    half_heads = pltpu.VMEM((n, half_rows, width), BF16)
    both_halves = pltpu.VMEM((2, n, half_rows, width), BF16)
    stream = pltpu.VMEM((rows, channels), BF16)
    hyena, by_heads = pl.pallas_call(
        functools.partial(fused, n, groups_per_tile, scale),
        out_shape=(
            jax.ShapeDtypeStruct(hyena_query.shape, BF16),
            jax.ShapeDtypeStruct((n, rows, width), BF16),
        ),
        in_specs=[hbm, hbm, hbm, vmem, hbm, hbm, hbm, hbm, hbm, hbm,
                  pl.BlockSpec(memory_space=pltpu.SMEM)],
        out_specs=(hbm, hbm),
        scratch_shapes=[
            stream, stream, stream, stream,
            pltpu.VMEM(context_tail.shape, BF16),
            pltpu.VMEM((2, rows, channels), BF16),
            pltpu.VMEM((groups, taps), F32),
            pltpu.VMEM((channels // 128, groups_per_tile * rows, 2 * rows), BF16),
            block, block, block, half_block, half_block,
            per_head, per_head, per_head, half_heads, half_heads,
            per_head, per_head, per_head, both_halves, both_halves,
            pltpu.VMEM((length_all, width), F32), pltpu.VMEM((length_all, width), F32),
            pltpu.VMEM((length_all, width), F32),
            per_head,
            pltpu.SemaphoreType.DMA((9,)), pltpu.SemaphoreType.DMA((9,)), pltpu.SemaphoreType.DMA((9,)),
        ],
        compiler_params=pltpu.CompilerParams(
            collective_id=0, has_side_effects=True, vmem_limit_bytes=63 * 2**20
        ),
        name="fused",
    )(
        hyena_query, hyena_key, hyena_value, hyena_filters, context_tail,
        cont_queries, cont_keys, cont_values, context_keys, context_values, lengths,
    )
    part = rows // 2
    hy_spec = pl.BlockSpec((1, part, channels), lambda i: (0, i, 0))
    return pl.pallas_call(
        finish,
        grid=(rows // part,),
        out_shape=(
            jax.ShapeDtypeStruct(hyena_query.shape, BF16),
            jax.ShapeDtypeStruct(cont_queries.shape, BF16),
        ),
        in_specs=[hy_spec, pl.BlockSpec((n, part, width), lambda i: (0, i, 0)),
                  pl.BlockSpec(memory_space=pltpu.SMEM)],
        out_specs=(hy_spec, pl.BlockSpec((1, part, heads, width), lambda i: (0, i, 0, 0))),
        name="finish",
    )(hyena, by_heads, lengths)


def solution(mesh):
    placed = (
        P("cand", "seq", None), P("cand", "seq", None), P("cand", "seq", None), P(), P(),
        P("cand", "seq", None, None), P("cand", "seq", None, None), P("cand", "seq", None, None),
        P("seq", None, None), P("seq", None, None), P("cand"),
    )
    return jax.shard_map(
        local, mesh=mesh, in_specs=placed,
        out_specs=(P("cand", "seq", None), P("cand", "seq", None, None)), check_vma=False,
    )
```

```python
import functools
import math

import jax
import jax.numpy as jnp
from jax import lax
from jax.experimental import pallas as pl
from jax.experimental.pallas import tpu as pltpu
from jax.sharding import PartitionSpec as P

F32 = jnp.float32
BF16 = jnp.bfloat16
MESH = pl.DeviceIdType.MESH
NT = (((1,), (1,)), ((), ()))
NN = (((1,), (0,)), ((), ()))
TN = (((0,), (0,)), ((), ()))
LOW = -1e30
RING = 4


def dot(a, b, dims):
    return lax.dot_general(a, b, dims, preferred_element_type=F32)


def leading_swap():
    to = lax.broadcasted_iota(jnp.int32, (256, 256), 0)
    source = lax.broadcasted_iota(jnp.int32, (256, 256), 1)
    return jnp.where(source == (to % 16) * 16 + to // 16, 1.0, 0.0).astype(BF16)


def finish(hy_ref, o_ref, len_ref, hy_out, att_ref):
    heads, rows, width = o_ref.shape
    total_rows = pl.num_programs(0) * rows
    start = lax.axis_index("seq") * total_rows + pl.program_id(0) * rows
    valid = len_ref[0] - start
    perm = leading_swap()
    row_of = lax.broadcasted_iota(jnp.int32, (256, width), 0) // 16
    for t in range(0, rows, 16):
        for h in range(0, heads, 16):
            tile = o_ref[h : h + 16, t : t + 16, :].reshape(256, width)
            kept = jnp.where(row_of < valid - t, dot(perm, tile, NN), 0.0).astype(BF16)
            att_ref[0, t : t + 16, h : h + 16, :] = kept.reshape(16, 16, width)
    hy_out[...] = hy_ref[...]


def fused(
    n, groups_per_tile, scale,
    hq_hbm, hk_hbm, hv_hbm, filt_ref, tail_hbm, q_hbm, k_hbm, v_hbm, ck_hbm, cv_hbm, len_ref,
    hy_hbm, o_in,
    hq, hk, hv, hy, tail, ext, ring, mats,
    q_in, k_in, v_in, ck_in, cv_in,
    q_out, k_out, v_out, ck_out, cv_out,
    q_all, k_all, v_all, ck_all, cv_all,
    m_s, l_s, acc_s, o_out,
    load_sem, send_sem, recv_sem,
):
    rows, heads, width = q_in.shape
    half_rows = ck_in.shape[0]
    length_all = n * rows
    me = lax.axis_index("seq")
    cand = lax.axis_index("cand")
    half = lax.rem(cand, 2)
    partner = cand + 1 - 2 * half

    barrier = pltpu.get_barrier_semaphore()

    def greet(i, _):
        pl.semaphore_signal(
            barrier, inc=1, device_id=(cand, lax.rem(me + i, n)), device_id_type=MESH
        )
        return 0

    lax.fori_loop(1, n, greet, 0)
    pl.semaphore_signal(barrier, inc=1, device_id=(partner, me), device_id_type=MESH)

    ctx_rows = pl.ds(half * half_rows, half_rows)
    loads = [
        pltpu.make_async_copy(ck_hbm.at[ctx_rows], ck_in, load_sem.at[0]),
        pltpu.make_async_copy(cv_hbm.at[ctx_rows], cv_in, load_sem.at[1]),
        pltpu.make_async_copy(q_hbm.at[0], q_in, load_sem.at[2]),
        pltpu.make_async_copy(k_hbm.at[0], k_in, load_sem.at[3]),
        pltpu.make_async_copy(v_hbm.at[0], v_in, load_sem.at[4]),
        pltpu.make_async_copy(hk_hbm.at[0], hk, load_sem.at[5]),
        pltpu.make_async_copy(hv_hbm.at[0], hv, load_sem.at[6]),
        pltpu.make_async_copy(hq_hbm.at[0], hq, load_sem.at[7]),
        pltpu.make_async_copy(tail_hbm, tail, load_sem.at[8]),
    ]
    for copy in loads:
        copy.start()

    perm = leading_swap()

    def by_head(src, dst):
        for t in range(0, src.shape[0], 16):
            for h in range(0, heads, 16):
                tile = src[t : t + 16, h : h + 16, :].reshape(256, width)
                turned_tile = dot(perm, tile, NN).astype(BF16)
                dst[h : h + 16, t : t + 16, :] = turned_tile.reshape(16, 16, width)

    column = me - lax.rem(me, RING)

    def scatter(src, dst_at, index):
        own = pltpu.make_async_copy(src.at[me], dst_at(me), recv_sem.at[index])
        own.start()

        def send(i):
            p = lax.rem(me + i, n)
            pltpu.make_async_remote_copy(
                src_ref=src.at[p], dst_ref=dst_at(me), send_sem=send_sem.at[index],
                recv_sem=recv_sem.at[index], device_id=(cand, p), device_id_type=MESH,
            ).start()

        lax.fori_loop(1, n, lambda i, _: (send(i), 0)[1], 0)

    def received(whole, index):
        pltpu.make_async_copy(whole, whole, recv_sem.at[index]).wait()

    def sent(part, index):
        pltpu.make_async_copy(part, part, send_sem.at[index]).wait()

    loads[0].wait()
    by_head(ck_in, ck_out)
    loads[1].wait()
    by_head(cv_in, cv_out)
    pl.semaphore_wait(barrier, n)
    scatter(ck_out, lambda s: ck_all.at[half, s], 0)
    scatter(cv_out, lambda s: cv_all.at[half, s], 1)
    loads[2].wait()
    by_head(q_in, q_out)
    scatter(q_out, lambda s: q_all.at[s], 2)
    loads[3].wait()
    by_head(k_in, k_out)
    scatter(k_out, lambda s: k_all.at[s], 3)
    loads[4].wait()
    by_head(v_in, v_out)
    scatter(v_out, lambda s: v_all.at[s], 4)

    loads[5].wait()
    loads[6].wait()
    ext[1] = (hk[...].astype(F32) * hv[...].astype(F32)).astype(BF16)

    def halo(to, piece):
        part = pl.ds(piece * 16, 16)
        return pltpu.make_async_remote_copy(
            src_ref=ext.at[1, part], dst_ref=ext.at[0, part], send_sem=send_sem.at[5],
            recv_sem=recv_sem.at[5], device_id=(cand, to), device_id_type=MESH,
        )

    @pl.when(me + 1 < n)
    def _():
        for piece in range(rows // 16):
            halo(me + 1, piece).start()

    loads[8].wait()

    taps = filt_ref.shape[0]
    turn_s = lax.broadcasted_iota(jnp.int32, (taps, taps), 0)
    turn_w = lax.broadcasted_iota(jnp.int32, (taps, taps), 1)
    turned = jnp.where((turn_s + turn_w) % taps == 0, 1.0, 0.0).astype(BF16)
    ring[...] = dot(filt_ref[...].astype(BF16), turned, TN)


    tiles = ext.shape[2] // 128
    out_row = lax.broadcasted_iota(jnp.int32, (rows, 128), 0)
    out_col = lax.broadcasted_iota(jnp.int32, (rows, 128), 1)
    before = out_col > out_row

    def filter_matrices(j, _):
        some = ring[pl.ds(pl.multiple_of(j * groups_per_tile, groups_per_tile), groups_per_tile), :]
        for g in range(groups_per_tile):
            line = jnp.broadcast_to(some[g : g + 1, :], (rows, 128))
            turns = pltpu.roll(line, 0, 1, stride=1, stride_axis=0)
            part = slice(g * rows, (g + 1) * rows)
            mats[j, part, :128] = jnp.where(before, turns, 0.0).astype(BF16)
            mats[j, part, 128:] = jnp.where(before, 0.0, turns).astype(BF16)
        return 0

    lax.fori_loop(0, tiles, filter_matrices, 0, unroll=2)

    received(ck_all.at[half], 0)
    received(cv_all.at[half], 1)
    swaps = []
    for index, ref in ((6, ck_all), (7, cv_all)):
        swap = pltpu.make_async_remote_copy(
            src_ref=ref.at[half], dst_ref=ref.at[half], send_sem=send_sem.at[index],
            recv_sem=recv_sem.at[index], device_id=(partner, me), device_id_type=MESH,
        )
        swap.start()
        swaps.append(swap)
    for swap in swaps:
        swap.wait_recv()
    received(q_all, 2)

    def spread(column):
        return jnp.broadcast_to(column, (column.shape[0], width))

    def fold(state, query_block, key_rows, value_rows, mask=None):
        m, l, acc = state
        s = dot(query_block, key_rows, NT)
        if mask is not None:
            s = jnp.where(mask, s, LOW)
        top = jnp.maximum(m, spread(jnp.max(s, axis=1, keepdims=True)))
        w = jnp.exp2((s - jnp.concatenate([top] * (s.shape[1] // width), axis=1)) * scale)
        shrink = jnp.exp2((m - top) * scale)
        l = l * shrink + spread(jnp.sum(w, axis=1, keepdims=True))
        acc = acc * shrink + dot(w.astype(BF16), value_rows, NN)
        return top, l, acc

    block = min(512, length_all)
    per_block = block // rows
    blocks = length_all // block
    ctx_total = 2 * n * half_rows
    ctx_step = 1024 if ctx_total % 1024 == 0 else ctx_total
    q_flat = q_all.reshape(length_all, width)
    k_flat = k_all.reshape(length_all, width)
    v_flat = v_all.reshape(length_all, width)
    ck_flat = ck_all.reshape(ctx_total, width)
    cv_flat = cv_all.reshape(ctx_total, width)

    def over_context(i, _):
        at = pl.ds(pl.multiple_of(i * block, block), block)
        query_block = q_flat[at, :]
        state = (
            jnp.full((block, width), LOW, F32), jnp.zeros((block, width), F32),
            jnp.zeros((block, width), F32),
        )
        for j in range(ctx_total // ctx_step):
            part = slice(j * ctx_step, (j + 1) * ctx_step)
            state = fold(state, query_block, ck_flat[part, :], cv_flat[part, :])
        m_s[at, :], l_s[at, :], acc_s[at, :] = state
        return 0

    lax.fori_loop(0, blocks, over_context, 0)

    received(k_all, 3)
    received(v_all, 4)

    o_flat = o_out.reshape(length_all, width)
    own_step = 2 * block
    ahead = lax.broadcasted_iota(jnp.int32, (block, own_step), 1) - lax.broadcasted_iota(
        jnp.int32, (block, own_step), 0
    )

    def over_own(index, full):
        at = pl.ds(pl.multiple_of(index * block, block), block)
        query_block = q_flat[at, :]
        state = (m_s[at, :], l_s[at, :], acc_s[at, :])
        for t in range(full + 1):
            part = slice(t * own_step, (t + 1) * own_step)
            mask = ahead <= index * block - full * own_step if t == full else None
            state = fold(state, query_block, k_flat[part, :], v_flat[part, :], mask)
        o_flat[at, :] = (state[2] / state[1]).astype(BF16)

    def over_pair(step, _):
        low = lax.rem(step + column // RING, blocks // 2)
        high = blocks - 1 - low
        for index, of_low in ((low, True), (high, False)):
            for g in range(blocks // 4):

                @pl.when(low // 2 == g)
                def _():
                    over_own(index, g if of_low else blocks // 2 - 1 - g)

            for r in range(per_block):
                p = index * per_block + r

                @pl.when(p != me)
                def _():
                    pltpu.make_async_remote_copy(
                        src_ref=o_out.at[p], dst_ref=o_in.at[me], send_sem=send_sem.at[8],
                        recv_sem=recv_sem.at[8], device_id=(cand, p), device_id_type=MESH,
                    ).start()
        return 0

    lax.fori_loop(0, blocks // 2, over_pair, 0)
    pltpu.make_async_copy(o_out.at[me], o_in.at[me], recv_sem.at[8]).start()

    @pl.when(me == 0)
    def _():
        def shift(j, _):
            cols = pl.ds(pl.multiple_of(j * 512, 512), 512)
            held = tail[:, cols].astype(F32)
            ext[0, :, cols] = jnp.concatenate([jnp.zeros((1, 512), F32), held], axis=0).astype(BF16)
            return 0

        lax.fori_loop(0, tail.shape[1] // 512, shift, 0)

    @pl.when(me > 0)
    def _():
        received(ext.at[0], 5)

    loads[7].wait()
    valid = len_ref[0] - me * rows
    keep = out_row < valid
    lane_group = out_col // (128 // groups_per_tile)

    def filtered(j, _):
        cols = pl.ds(pl.multiple_of(j * 128, 128), 128)
        stream = jnp.concatenate([ext[0, :, cols], ext[1, :, cols]], axis=0)
        every = dot(mats[j], stream, NN)
        mixed = every[:rows]
        for g in range(1, groups_per_tile):
            mixed = jnp.where(lane_group == g, every[g * rows : (g + 1) * rows], mixed)
        gated = jnp.where(keep, hq[:, cols].astype(F32) * mixed, 0.0)
        hy[:, cols] = gated.astype(BF16)
        return 0

    lax.fori_loop(0, tiles, filtered, 0, unroll=4)

    store = pltpu.make_async_copy(hy, hy_hbm.at[0], load_sem.at[7])
    store.start()

    received(o_in, 8)
    store.wait()
    for index, ref in ((0, ck_out), (1, cv_out), (4, v_out), (8, o_out)):
        sent(ref.at[pl.ds(0, n - 1)], index)
    for index, ref in ((2, q_out), (3, k_out)):
        sent(ref.at[pl.ds(0, n - 1)], index)

    @pl.when(me + 1 < n)
    def _():
        sent(ext.at[1], 5)

    for swap in swaps:
        swap.wait_send()


def local(
    hyena_query, hyena_key, hyena_value, hyena_filters, context_tail,
    cont_queries, cont_keys, cont_values, context_keys, context_values, lengths,
):
    n = lax.axis_size("seq")
    _, rows, channels = hyena_key.shape
    heads, width = cont_queries.shape[2:]
    half_rows = context_keys.shape[0] // 2
    taps, groups = hyena_filters.shape
    groups_per_tile = 128 * groups // channels
    length_all = n * rows
    scale = math.log2(math.e) / math.sqrt(width)
    hbm = pl.BlockSpec(memory_space=pl.ANY)
    vmem = pl.BlockSpec(memory_space=pltpu.VMEM)
    block = pltpu.VMEM((rows, heads, width), BF16)
    per_head = pltpu.VMEM((n, rows, width), BF16)
    half_block = pltpu.VMEM((half_rows, heads, width), BF16)
    half_heads = pltpu.VMEM((n, half_rows, width), BF16)
    both_halves = pltpu.VMEM((2, n, half_rows, width), BF16)
    stream = pltpu.VMEM((rows, channels), BF16)
    hyena, by_heads = pl.pallas_call(
        functools.partial(fused, n, groups_per_tile, scale),
        out_shape=(
            jax.ShapeDtypeStruct(hyena_query.shape, BF16),
            jax.ShapeDtypeStruct((n, rows, width), BF16),
        ),
        in_specs=[hbm, hbm, hbm, vmem, hbm, hbm, hbm, hbm, hbm, hbm,
                  pl.BlockSpec(memory_space=pltpu.SMEM)],
        out_specs=(hbm, hbm),
        scratch_shapes=[
            stream, stream, stream, stream,
            pltpu.VMEM(context_tail.shape, BF16),
            pltpu.VMEM((2, rows, channels), BF16),
            pltpu.VMEM((groups, taps), F32),
            pltpu.VMEM((channels // 128, groups_per_tile * rows, 2 * rows), BF16),
            block, block, block, half_block, half_block,
            per_head, per_head, per_head, half_heads, half_heads,
            per_head, per_head, per_head, both_halves, both_halves,
            pltpu.VMEM((length_all, width), F32), pltpu.VMEM((length_all, width), F32),
            pltpu.VMEM((length_all, width), F32),
            per_head,
            pltpu.SemaphoreType.DMA((9,)), pltpu.SemaphoreType.DMA((9,)), pltpu.SemaphoreType.DMA((9,)),
        ],
        compiler_params=pltpu.CompilerParams(
            collective_id=0, has_side_effects=True, vmem_limit_bytes=63 * 2**20
        ),
        name="fused",
    )(
        hyena_query, hyena_key, hyena_value, hyena_filters, context_tail,
        cont_queries, cont_keys, cont_values, context_keys, context_values, lengths,
    )
    part = rows // 2
    hy_spec = pl.BlockSpec((1, part, channels), lambda i: (0, i, 0))
    return pl.pallas_call(
        finish,
        grid=(rows // part,),
        out_shape=(
            jax.ShapeDtypeStruct(hyena_query.shape, BF16),
            jax.ShapeDtypeStruct(cont_queries.shape, BF16),
        ),
        in_specs=[hy_spec, pl.BlockSpec((n, part, width), lambda i: (0, i, 0)),
                  pl.BlockSpec(memory_space=pltpu.SMEM)],
        out_specs=(hy_spec, pl.BlockSpec((1, part, heads, width), lambda i: (0, i, 0, 0))),
        name="finish",
    )(hyena, by_heads, lengths)


def solution(mesh):
    placed = (
        P("cand", "seq", None), P("cand", "seq", None), P("cand", "seq", None), P(), P(),
        P("cand", "seq", None, None), P("cand", "seq", None, None), P("cand", "seq", None, None),
        P("seq", None, None), P("seq", None, None), P("cand"),
    )
    return jax.shard_map(
        local, mesh=mesh, in_specs=placed,
        out_specs=(P("cand", "seq", None), P("cand", "seq", None, None)), check_vma=False,
    )
```
